32 devices in a mesh: segment: 2 (over y), ctx: 16 (over z, x, core).
Axes of the slice: x: 2, y: 2, z: 4, core: 2. Of those that a mesh axis runs over, the one named last changes fastest.
Arguments:
- queries: bfloat16 [2, 2, 6144, 2048], P('segment', None, 'ctx'), may hold values from -60 to 60
- enc_keys_values: bfloat16 [2, 2, 6144, 2048], P(None, None, 'ctx'), may hold values from -6 to 6
- mem_map: bfloat16 [32, 64, 128], replicated, may hold values from -0.75 to 0.75
Outputs:
- contexts: bfloat16 [2, 2, 6144, 2048], P('segment', None, 'ctx')
The draws below stay inside these ranges and needn't reach their ends.
All inputs are finite; a program needn't handle non-finite values.
Results may differ from the reference program's by a relative error of at most 0.0058.
Values may be sent and summed in bfloat16 or wider, within the bound.
A program may use at most 128 MiB of HBM per device.

```python
import jax
import jax.numpy as jnp
from jax import lax

HEADS = 32
DH = 64
HD = 2048
TOK_DEV = 384
MB = 2
SEQ = 6144
N_CTX = 16


def drawn_pair(key):
    query_key = jax.random.fold_in(key, 101)
    pair_key = jax.random.fold_in(key, 202)
    queries = jax.random.truncated_normal(query_key, -6.0, 6.0, (2, MB, SEQ, HD), jnp.float32)
    pairs = jax.random.truncated_normal(pair_key, -6.0, 6.0, (MB, 2, SEQ, HD), jnp.float32)
    return (queries, pairs)


def draw_queries(key, part):
    queries, pairs = drawn_pair(key)
    return queries.astype(jnp.bfloat16)


def draw_enc_keys_values(key, part):
    queries, pairs = drawn_pair(key)
    return pairs.astype(jnp.bfloat16)


def centred(own_key, dims, scale, limit, kind=jnp.bfloat16):
    return jnp.clip(scale * jax.random.normal(own_key, dims, jnp.float32), -limit, limit).astype(kind)


def setup_inputs(seed: int = 0) -> dict:
    streams_of = jax.random.split(jax.random.key(seed), 4)
    queries = draw_queries(jax.random.fold_in(streams_of[3], 71), 0)
    enc_keys_values = draw_enc_keys_values(jax.random.fold_in(streams_of[3], 71), 0)
    mem_map = centred(streams_of[2], (HEADS, DH, 2 * DH), DH ** -0.5, 0.75)
    return dict(queries=queries, enc_keys_values=enc_keys_values, mem_map=mem_map)


def attend_block(query_rows, key_rows, value_rows):
    query_count = query_rows.shape[0]
    key_count = key_rows.shape[0]
    query_heads = query_rows.astype(jnp.float32).reshape(query_count, HEADS, DH)
    key_heads = key_rows.astype(jnp.float32).reshape(key_count, HEADS, DH)
    value_heads = value_rows.astype(jnp.float32).reshape(key_count, HEADS, DH)
    scores = jnp.einsum('qhd,khd->hqk', query_heads, key_heads) * (1.0 / DH ** 0.5)
    row_max = lax.optimization_barrier(jnp.max(scores, axis=2, keepdims=True))
    powers = jnp.exp(scores - row_max)
    totals = lax.optimization_barrier(jnp.sum(powers, axis=2))
    weights = powers.astype(jnp.bfloat16)
    weights = lax.optimization_barrier(weights).astype(jnp.float32)
    summed = jnp.einsum('hqk,khd->qhd', weights, value_heads)
    result = summed / jnp.transpose(totals)[:, :, None]
    return result.reshape(query_count, HEADS * DH).astype(jnp.bfloat16)

def windows(array):
    blocked = array.reshape(N_CTX, TOK_DEV, HD)
    return jnp.concatenate((jnp.roll(blocked, 1, axis=0), blocked, jnp.roll(blocked, -1, axis=0)), axis=1)

def blockwise(query_all, key_all, value_all):
    query_blocks = query_all.reshape(N_CTX, TOK_DEV, HD)
    key_windows = windows(key_all)
    value_windows = windows(value_all)

    def one_block(items):
        return attend_block(items[0], items[1], items[2])
    result = lax.map(one_block, (query_blocks, key_windows, value_windows))
    return result.reshape(N_CTX * TOK_DEV, HD)

def build(key_value, context, mem_map):
    row_count = context.shape[0]
    floated = context.astype(jnp.float32)
    root_mean = jnp.sqrt(lax.optimization_barrier(jnp.mean(floated * floated, axis=1, keepdims=True)) + 1e-06)
    normed = (floated / root_mean).astype(jnp.bfloat16)
    normed = lax.optimization_barrier(normed).astype(jnp.float32).reshape(row_count, HEADS, DH)
    mapped = jnp.einsum('rhd,hde->rhe', normed, mem_map.astype(jnp.float32))
    key_part = mapped[:, :, :DH].reshape(row_count, HEADS * DH)
    value_part = mapped[:, :, DH:].reshape(row_count, HEADS * DH)
    new_keys = key_value[0].astype(jnp.float32) + key_part
    new_values = key_value[1].astype(jnp.float32) + value_part
    return jnp.stack((new_keys, new_values)).astype(jnp.bfloat16)

def reference(queries, enc_keys_values, mem_map):
    encoder_out = []
    decoder_out = []
    for batch_index in range(MB):
        key_value = enc_keys_values[batch_index]
        encoder_context = blockwise(queries[0, batch_index], key_value[0], key_value[1])
        memory = build(key_value, encoder_context, mem_map)
        decoder_context = blockwise(queries[1, batch_index], memory[0], memory[1])
        encoder_out.append(encoder_context)
        decoder_out.append(decoder_context)
    return jnp.stack((jnp.stack(encoder_out), jnp.stack(decoder_out)))
```

```python
import functools

import jax
import jax.numpy as jnp
from jax import lax
from jax.experimental import pallas as pl
from jax.experimental.pallas import tpu as pltpu
from jax.sharding import PartitionSpec as P

LANES = 128
CHUNKS = 4


def attend_pair(query, keys, values, head_size):
    rows = query.shape[0]
    scale = head_size ** -0.5
    low = lax.broadcasted_iota(jnp.int32, (1, LANES), 1) < head_size
    scaled = query * jnp.asarray(scale, query.dtype)
    one = jnp.ones((), query.dtype)
    zero = jnp.zeros((), query.dtype)
    values_of = (
        [jnp.where(low, v, one) for v in values],
        [jnp.where(low, one, v) for v in values],
    )
    queries_of = (jnp.where(low, scaled, zero), jnp.where(low, zero, scaled))
    tile = 128
    out = []
    for start in range(0, rows, tile):
        sums = []
        for head in range(2):
            part = queries_of[head][start : start + tile]
            scores = [
                lax.dot_general(
                    part, k, (((1,), (1,)), ((), ())), preferred_element_type=jnp.float32
                )
                for k in keys
            ]
            top = functools.reduce(jnp.maximum, [jnp.max(s, axis=1, keepdims=True) for s in scores])
            total = None
            for s, v in zip(scores, values_of[head]):
                weights = jnp.exp(s - top).astype(jnp.bfloat16)
                term = jnp.dot(weights, v, preferred_element_type=jnp.float32)
                total = term if total is None else total + term
            sums.append(total)
        above = jnp.where(low, sums[0], sums[1])
        below = pltpu.roll(jnp.where(low, sums[1], sums[0]), head_size, 1)
        out.append((above / below).astype(jnp.bfloat16))
    return jnp.concatenate(out, axis=0)


def encoder_kernel(head_size, which, own_q, other_q, own, near, far, out):
    first = which[0] == 0
    query = jnp.where(first, own_q[0, 0], other_q[...])
    keys = [own[0, 0], near[0], far[0]]
    values = [own[0, 1], near[1], far[1]]
    out[...] = attend_pair(query, keys, values, head_size)


def decoder_kernel(
    head_size, which, own_q, other_q, own, near, far, own_c, near_c, far_c, roots, maps, out
):
    first = which[0] == 0
    query = jnp.where(first, other_q[...], own_q[0, 0])
    keys, values = [], []
    sides = ((own[0, 0], own[0, 1], own_c), (near[0], near[1], near_c), (far[0], far[1], far_c))
    for index, (key, value, context) in enumerate(sides):
        normed = (context[...].astype(jnp.float32) / roots[index]).astype(jnp.bfloat16)
        mapped = jnp.dot(normed, maps[0], preferred_element_type=jnp.float32)
        keys.append((key.astype(jnp.float32) + mapped[:, :LANES]).astype(jnp.bfloat16))
        values.append((value.astype(jnp.float32) + mapped[:, LANES:]).astype(jnp.bfloat16))
    out[...] = attend_pair(query, keys, values, head_size)


def root_kernel(count, channels, *refs):
    out = refs[-1]
    for index in range(3):
        total = None
        for c in refs[index * count : (index + 1) * count]:
            x = c[...].astype(jnp.float32)
            part = jnp.sum(x * x, axis=1, keepdims=True)
            total = part if total is None else total + part
        out[index] = jnp.sqrt(total / channels + 1e-06)


def body(queries, enc_keys_values, mem_map):
    heads, head_size = mem_map.shape[0], mem_map.shape[1]
    batches, rows, channels = (
        enc_keys_values.shape[0],
        enc_keys_values.shape[2],
        enc_keys_values.shape[3],
    )
    width = channels // CHUNKS
    pairs = width // LANES
    segment = lax.axis_index("segment")
    size = lax.axis_size("ctx")
    swap = [(0, 1), (1, 0)]
    near_pairs = [(i, i ^ 1) for i in range(size)]
    far_pairs = [(i, (i + 1) % size if i % 2 else (i - 1) % size) for i in range(size)]
    which = segment.astype(jnp.int32)[None]

    def cut(array, index, chunk):
        start = (index,) + (0,) * (array.ndim - 2) + (chunk * width,)
        sizes = (1,) + array.shape[1:-1] + (width,)
        return lax.dynamic_slice(array, start, sizes)[0]

    own_queries = queries[0]
    near_kv, far_kv, other_q = [], [], []
    for g in range(CHUNKS):
        block = cut(enc_keys_values, segment, g)
        far_kv.append(lax.ppermute(block, "ctx", far_pairs))
        near_kv.append(lax.ppermute(block, "ctx", near_pairs))
        other_q.append(lax.ppermute(cut(own_queries, 1 - segment, g), "segment", swap))

    def specs(g):
        base = g * pairs
        return [
            pl.BlockSpec((1, 1, rows, LANES), lambda i, w: (0, w[0], 0, base + i)),
            pl.BlockSpec((rows, LANES), lambda i, w: (0, i)),
            pl.BlockSpec((1, 2, rows, LANES), lambda i, w: (w[0], 0, 0, base + i)),
            pl.BlockSpec((2, rows, LANES), lambda i, w: (0, 0, i)),
            pl.BlockSpec((2, rows, LANES), lambda i, w: (0, 0, i)),
        ]

    cost = pl.CostEstimate(
        flops=2 * 2 * rows * 3 * rows * width,
        bytes_accessed=2 * 8 * rows * width,
        transcendentals=rows * 3 * rows * width // head_size,
    )
    params = pltpu.CompilerParams(vmem_limit_bytes=40 << 20)
    tile = pl.BlockSpec((rows, LANES), lambda i, w: (0, i))

    def encode(g):
        return pl.pallas_call(
            functools.partial(encoder_kernel, head_size),
            name="encode",
            out_shape=jax.ShapeDtypeStruct((rows, width), jnp.bfloat16),
            grid_spec=pltpu.PrefetchScalarGridSpec(
                num_scalar_prefetch=1, grid=(pairs,), in_specs=specs(g), out_specs=tile
            ),
            compiler_params=params,
            cost_estimate=cost,
        )(which, queries, other_q[g], enc_keys_values, near_kv[g], far_kv[g])

    own_c, near_c, far_c, enc_other = [], [], [], []
    for g in range(CHUNKS):
        context = encode(g)
        own_c.append(context)
        far_c.append(lax.ppermute(context, "ctx", far_pairs))
        near_c.append(lax.ppermute(context, "ctx", near_pairs))
        enc_other.append(lax.ppermute(context, "segment", [(1, 0)]))

    roots = pl.pallas_call(
        functools.partial(root_kernel, CHUNKS, channels),
        name="roots",
        out_shape=jax.ShapeDtypeStruct((3, rows, 1), jnp.float32),
    )(*own_c, *near_c, *far_c)

    split = mem_map.reshape(heads // 2, 2, head_size, 2, head_size)
    eye = jnp.eye(2, dtype=mem_map.dtype)
    maps = (
        (split.transpose(0, 1, 2, 3, 4)[:, :, :, :, None, :] * eye[None, :, None, None, :, None])
        .reshape(heads // 2, LANES, 2 * LANES)
        .astype(jnp.bfloat16)
    )

    def decode(g):
        base = g * pairs
        return pl.pallas_call(
            functools.partial(decoder_kernel, head_size),
            name="decode",
            out_shape=jax.ShapeDtypeStruct((rows, width), jnp.bfloat16),
            grid_spec=pltpu.PrefetchScalarGridSpec(
                num_scalar_prefetch=1,
                grid=(pairs,),
                in_specs=specs(g)
                + [tile, tile, tile]
                + [
                    pl.BlockSpec((3, rows, 1), lambda i, w: (0, 0, 0)),
                    pl.BlockSpec((1, LANES, 2 * LANES), lambda i, w: (base + i, 0, 0)),
                ],
                out_specs=tile,
            ),
            compiler_params=params,
            cost_estimate=cost,
        )(
            which, queries, other_q[g], enc_keys_values, near_kv[g], far_kv[g],
            own_c[g], near_c[g], far_c[g], roots, maps,
        )

    own_d, dec_other = [], []
    for g in range(CHUNKS):
        context = decode(g)
        own_d.append(context)
        dec_other.append(lax.ppermute(context, "segment", [(0, 1)]))

    first = segment == 0
    slots = []
    slots.append(
        jnp.concatenate([jnp.where(first, a, b) for a, b in zip(own_c, dec_other)], axis=1)
    )
    slots.append(
        jnp.concatenate([jnp.where(first, a, b) for a, b in zip(enc_other, own_d)], axis=1)
    )
    return jnp.stack(slots)[None]


def solution(mesh):
    in_specs = (P("segment", None, "ctx", None), P(None, None, "ctx", None), P())
    out_specs = P("segment", None, "ctx", None)
    return jax.shard_map(body, mesh=mesh, in_specs=in_specs, out_specs=out_specs, check_vma=False)
```

```python
import functools

import jax
import jax.numpy as jnp
from jax import lax
from jax.experimental import pallas as pl
from jax.experimental.pallas import tpu as pltpu
from jax.sharding import PartitionSpec as P

LANES = 128
CHUNKS = 4
GROUP = 2
TILE = 64
GATE = 0
VMEM_LIMIT = 56 << 20


def attend_pair(query, keys, values, head_size, scores):
    rows = query.shape[0]
    low = lax.broadcasted_iota(jnp.int32, (1, LANES), 1) < head_size
    scaled = query * jnp.asarray(head_size**-0.5, query.dtype)
    one = jnp.ones((), query.dtype)
    zero = jnp.zeros((), query.dtype)
    queries_of = (jnp.where(low, scaled, zero), jnp.where(low, zero, scaled))
    values_of = (jnp.where(low, values, one), jnp.where(low, one, values))
    for head in range(2):
        scores[head][...] = lax.dot_general(
            queries_of[head], keys, (((1,), (1,)), ((), ())), preferred_element_type=jnp.float32
        )
    sums = []
    for head in range(2):
        weights = []
        for start in range(0, rows, TILE):
            part = scores[head][start : start + TILE, :]
            top = jnp.max(part, axis=1, keepdims=True)
            weights.append(jnp.exp(part - top).astype(jnp.bfloat16))
        sums.append(
            jnp.dot(
                jnp.concatenate(weights, axis=0),
                values_of[head],
                preferred_element_type=jnp.float32,
            )
        )
    above = jnp.where(low, sums[0], sums[1])
    below = pltpu.roll(jnp.where(low, sums[1], sums[0]), head_size, 1)
    return (above / below).astype(jnp.bfloat16)


def lanes_of(pair):
    return slice(pair * LANES, (pair + 1) * LANES)


def encoder_kernel(head_size, which, own_q, other_q, own, near, far, out, *scores):
    first = which[0] == 0
    for pair in range(GROUP):
        c = lanes_of(pair)
        query = jnp.where(first, own_q[0, 0, :, c], other_q[:, c])
        keys = jnp.concatenate([own[0, 0, :, c], near[0, :, c], far[0, :, c]], axis=0)
        values = jnp.concatenate([own[0, 1, :, c], near[1, :, c], far[1, :, c]], axis=0)
        out[:, c] = attend_pair(query, keys, values, head_size, scores[2 * pair : 2 * pair + 2])


def decoder_kernel(
    head_size, which, own_q, other_q, own, near, far, own_c, near_c, far_c, roots, maps, *rest
):
    keep, send, scores = rest[-2 * GROUP - 2], rest[-2 * GROUP - 1], rest[-2 * GROUP :]
    first = which[0] == 0
    upper = lax.broadcasted_iota(jnp.int32, (LANES, 1), 0) < head_size
    low = lax.broadcasted_iota(jnp.int32, (1, LANES), 1) < head_size
    for pair in range(GROUP):
        c = lanes_of(pair)
        query = jnp.where(first, other_q[:, c], own_q[0, 0, :, c])
        both = maps[pair].astype(jnp.float32)
        turned = pltpu.roll(both, head_size, 1)
        key_map = jnp.where(upper & low, both, jnp.where(upper | low, 0.0, turned))
        value_map = jnp.where(upper & low, turned, jnp.where(upper | low, 0.0, both))
        joint = jnp.concatenate([key_map, value_map], axis=1).astype(jnp.bfloat16)
        keys, values = [], []
        sides = (
            (own[0, 0, :, c], own[0, 1, :, c], own_c),
            (near[0, :, c], near[1, :, c], near_c),
            (far[0, :, c], far[1, :, c], far_c),
        )
        for index, (key, value, context) in enumerate(sides):
            normed = (context[:, c].astype(jnp.float32) / roots[index]).astype(jnp.bfloat16)
            mapped = jnp.dot(normed, joint, preferred_element_type=jnp.float32)
            keys.append((key.astype(jnp.float32) + mapped[:, :LANES]).astype(jnp.bfloat16))
            values.append((value.astype(jnp.float32) + mapped[:, LANES:]).astype(jnp.bfloat16))
        result = attend_pair(
            query,
            jnp.concatenate(keys, axis=0),
            jnp.concatenate(values, axis=0),
            head_size,
            scores[2 * pair : 2 * pair + 2],
        )
        encoded = own_c[:, c]
        keep[0, 0, :, c] = jnp.where(first, encoded, result)
        send[:, c] = jnp.where(first, result, encoded)


def root_kernel(count, channels, *refs):
    out = refs[-1]
    for index in range(3):
        total = None
        for c in refs[index * count : (index + 1) * count]:
            x = c[...].astype(jnp.float32)
            part = jnp.sum(x * x, axis=1, keepdims=True)
            total = part if total is None else total + part
        out[index] = jnp.sqrt(total / channels + 1e-06)


def body(queries, enc_keys_values, mem_map):
    heads, head_size = mem_map.shape[0], mem_map.shape[1]
    batches, rows, channels = (
        enc_keys_values.shape[0],
        enc_keys_values.shape[2],
        enc_keys_values.shape[3],
    )
    width = channels // CHUNKS
    pairs = width // LANES
    segment = lax.axis_index("segment")
    size = lax.axis_size("ctx")
    swap = [(0, 1), (1, 0)]
    near_pairs = [(i, i ^ 1) for i in range(size)]
    far_pairs = [(i, (i + 1) % size if i % 2 else (i - 1) % size) for i in range(size)]
    which = segment.astype(jnp.int32)[None]

    def cut(array, index, chunk):
        start = (index,) + (0,) * (array.ndim - 2) + (chunk * width,)
        sizes = (1,) + array.shape[1:-1] + (width,)
        return lax.dynamic_slice(array, start, sizes)[0]

    own_queries = queries[0]
    near_kv, far_kv, other_q = [], [], []
    for g in range(CHUNKS):
        block = cut(enc_keys_values, segment, g)
        if GATE and g >= GATE:
            block, far_kv[g - GATE] = lax.optimization_barrier((block, far_kv[g - GATE]))
        far_kv.append(lax.ppermute(block, "ctx", far_pairs))
        near_kv.append(lax.ppermute(block, "ctx", near_pairs))
        other_q.append(lax.ppermute(cut(own_queries, 1 - segment, g), "segment", swap))

    step = GROUP * LANES
    steps = width // step

    def specs(g):
        base = g * steps
        return [
            pl.BlockSpec((1, 1, rows, step), lambda i, w: (0, w[0], 0, base + i)),
            pl.BlockSpec((rows, step), lambda i, w: (0, i)),
            pl.BlockSpec((1, 2, rows, step), lambda i, w: (w[0], 0, 0, base + i)),
            pl.BlockSpec((2, rows, step), lambda i, w: (0, 0, i)),
            pl.BlockSpec((2, rows, step), lambda i, w: (0, 0, i)),
        ]

    cost = pl.CostEstimate(
        flops=2 * 2 * rows * 3 * rows * width,
        bytes_accessed=2 * 8 * rows * width,
        transcendentals=rows * 3 * rows * width // head_size,
    )
    params = pltpu.CompilerParams(vmem_limit_bytes=VMEM_LIMIT)
    tile = pl.BlockSpec((rows, step), lambda i, w: (0, i))
    scores = [pltpu.VMEM((rows, 3 * rows), jnp.float32)] * (2 * GROUP)

    def encode(g):
        return pl.pallas_call(
            functools.partial(encoder_kernel, head_size),
            name="encode",
            out_shape=jax.ShapeDtypeStruct((rows, width), jnp.bfloat16),
            grid_spec=pltpu.PrefetchScalarGridSpec(
                num_scalar_prefetch=1,
                grid=(steps,),
                in_specs=specs(g),
                out_specs=tile,
                scratch_shapes=scores,
            ),
            compiler_params=params,
            cost_estimate=cost,
        )(which, queries, other_q[g], enc_keys_values, near_kv[g], far_kv[g])

    own_c, near_c, far_c = [], [], []
    for g in range(CHUNKS):
        context = encode(g)
        own_c.append(context)
        far_c.append(lax.ppermute(context, "ctx", far_pairs))
        near_c.append(lax.ppermute(context, "ctx", near_pairs))

    roots = pl.pallas_call(
        functools.partial(root_kernel, CHUNKS, channels),
        name="roots",
        out_shape=jax.ShapeDtypeStruct((3, rows, 1), jnp.float32),
    )(*own_c, *near_c, *far_c)
    maps = mem_map.reshape(heads // 2, LANES, 2 * head_size)

    def decode(g, final):
        base = g * steps
        operands = [
            which, queries, other_q[g], enc_keys_values, near_kv[g], far_kv[g],
            own_c[g], near_c[g], far_c[g], roots, maps,
        ]
        in_specs = specs(g) + [
            tile,
            tile,
            tile,
            pl.BlockSpec((3, rows, 1), lambda i, w: (0, 0, 0)),
            pl.BlockSpec((GROUP, LANES, LANES), lambda i, w: (base + i, 0, 0)),
        ]
        aliases = {}
        if final is not None:
            aliases = {len(operands): 0}
            operands.append(final)
            in_specs.append(pl.BlockSpec(memory_space=pl.ANY))
        return pl.pallas_call(
            functools.partial(decoder_kernel, head_size),
            name="decode",
            out_shape=(
                jax.ShapeDtypeStruct((1, batches, rows, channels), jnp.bfloat16),
                jax.ShapeDtypeStruct((rows, width), jnp.bfloat16),
            ),
            grid_spec=pltpu.PrefetchScalarGridSpec(
                num_scalar_prefetch=1,
                grid=(steps,),
                in_specs=in_specs,
                out_specs=(
                    pl.BlockSpec((1, 1, rows, step), lambda i, w: (0, w[0], 0, base + i)),
                    tile,
                ),
                scratch_shapes=scores,
            ),
            input_output_aliases=aliases,
            compiler_params=params,
            cost_estimate=cost,
        )(*operands)

    final, arrived = None, []
    for g in range(CHUNKS):
        final, send = decode(g, final)
        arrived.append(lax.ppermute(send, "segment", swap))
    for g in range(CHUNKS):
        final = lax.dynamic_update_slice(
            final, arrived[g][None, None], (0, 1 - segment, 0, g * width)
        )
    return final


def solution(mesh):
    in_specs = (P("segment", None, "ctx", None), P(None, None, "ctx", None), P())
    out_specs = P("segment", None, "ctx", None)
    return jax.shard_map(body, mesh=mesh, in_specs=in_specs, out_specs=out_specs, check_vma=False)
```

```python
import functools

import jax
import jax.numpy as jnp
from jax import lax
from jax.experimental import pallas as pl
from jax.experimental.pallas import tpu as pltpu
from jax.sharding import PartitionSpec as P


LANES = 128
CHUNKS = 4
GROUP = 2
TILE = 64
GATE = 0
VMEM_LIMIT = 56 << 20


def attend_pair(query, keys, values, head_size, scores, state=None):
    rows = query.shape[0]
    low = lax.broadcasted_iota(jnp.int32, (1, LANES), 1) < head_size
    scaled = query * jnp.asarray(head_size**-0.5, query.dtype)
    one = jnp.ones((), query.dtype)
    zero = jnp.zeros((), query.dtype)
    queries_of = (jnp.where(low, scaled, zero), jnp.where(low, zero, scaled))
    values_of = (jnp.where(low, values, one), jnp.where(low, one, values))
    for head in range(2):
        scores[head][...] = lax.dot_general(
            queries_of[head], keys, (((1,), (1,)), ((), ())), preferred_element_type=jnp.float32
        )
    sums, tops = [], []
    for head in range(2):
        weights, highest = [], []
        for start in range(0, rows, TILE):
            part = scores[head][start : start + TILE, :]
            top = jnp.max(part, axis=1, keepdims=True)
            if state is not None:
                top = jnp.maximum(top, state[1][head][start : start + TILE])
            highest.append(top)
            weights.append(jnp.exp(part - top).astype(jnp.bfloat16))
        total = jnp.dot(
            jnp.concatenate(weights, axis=0), values_of[head], preferred_element_type=jnp.float32
        )
        top = jnp.concatenate(highest, axis=0)
        if state is not None:
            total = total + state[0][head] * jnp.exp(state[1][head] - top)
        sums.append(total)
        tops.append(top)
    return sums, tops


def joined(sums, head_size):
    low = lax.broadcasted_iota(jnp.int32, (1, LANES), 1) < head_size
    above = jnp.where(low, sums[0], sums[1])
    below = pltpu.roll(jnp.where(low, sums[1], sums[0]), head_size, 1)
    return (above / below).astype(jnp.bfloat16)


def put_state(ref, pair, sums, tops, head_size):
    low = lax.broadcasted_iota(jnp.int32, (1, LANES), 1) < head_size
    base = pair * 3 * LANES
    ref[:, base : base + LANES] = sums[0]
    ref[:, base + LANES : base + 2 * LANES] = sums[1]
    ref[:, base + 2 * LANES : base + 3 * LANES] = jnp.where(low, tops[0], tops[1])


def get_state(ref, pair, head_size):
    base = pair * 3 * LANES
    tops = ref[:, base + 2 * LANES : base + 3 * LANES]
    return (
        (ref[:, base : base + LANES], ref[:, base + LANES : base + 2 * LANES]),
        (tops[:, :1], tops[:, head_size : head_size + 1]),
    )


def lanes_of(pair):
    return slice(pair * LANES, (pair + 1) * LANES)


def encode_near(head_size, which, own_q, other_q, own, near, state, *scores):
    first = which[0] == 0
    for pair in range(GROUP):
        c = lanes_of(pair)
        query = jnp.where(first, own_q[0, 0, :, c], other_q[:, c])
        keys = jnp.concatenate([own[0, 0, :, c], near[0, :, c]], axis=0)
        values = jnp.concatenate([own[0, 1, :, c], near[1, :, c]], axis=0)
        part = scores[2 * pair : 2 * pair + 2]
        sums, tops = attend_pair(query, keys, values, head_size, part)
        put_state(state, pair, sums, tops, head_size)


def encode_far(head_size, which, own_q, other_q, far, state, out, *scores):
    first = which[0] == 0
    for pair in range(GROUP):
        c = lanes_of(pair)
        query = jnp.where(first, own_q[0, 0, :, c], other_q[:, c])
        part = scores[2 * pair : 2 * pair + 2]
        earlier = get_state(state, pair, head_size)
        sums, _ = attend_pair(query, far[0, :, c], far[1, :, c], head_size, part, earlier)
        out[:, c] = joined(sums, head_size)


def joint_map(both, head_size):
    upper = lax.broadcasted_iota(jnp.int32, (LANES, 1), 0) < head_size
    low = lax.broadcasted_iota(jnp.int32, (1, LANES), 1) < head_size
    both = both.astype(jnp.float32)
    turned = pltpu.roll(both, head_size, 1)
    key_map = jnp.where(upper & low, both, jnp.where(upper | low, 0.0, turned))
    value_map = jnp.where(upper & low, turned, jnp.where(upper | low, 0.0, both))
    return jnp.concatenate([key_map, value_map], axis=1).astype(jnp.bfloat16)


def memory_of(key, value, context, root, joint):
    normed = (context.astype(jnp.float32) / root).astype(jnp.bfloat16)
    mapped = jnp.dot(normed, joint, preferred_element_type=jnp.float32)
    return (
        (key.astype(jnp.float32) + mapped[:, :LANES]).astype(jnp.bfloat16),
        (value.astype(jnp.float32) + mapped[:, LANES:]).astype(jnp.bfloat16),
    )


def decode_near(
    head_size, which, own_q, other_q, own, near, own_c, near_c, own_r, near_r, maps, state, *scores
):
    first = which[0] == 0
    for pair in range(GROUP):
        c = lanes_of(pair)
        query = jnp.where(first, other_q[:, c], own_q[0, 0, :, c])
        joint = joint_map(maps[pair], head_size)
        one = memory_of(own[0, 0, :, c], own[0, 1, :, c], own_c[:, c], own_r[...], joint)
        two = memory_of(near[0, :, c], near[1, :, c], near_c[:, c], near_r[...], joint)
        keys = jnp.concatenate([one[0], two[0]], axis=0)
        values = jnp.concatenate([one[1], two[1]], axis=0)
        part = scores[2 * pair : 2 * pair + 2]
        sums, tops = attend_pair(query, keys, values, head_size, part)
        put_state(state, pair, sums, tops, head_size)


def decode_far(
    head_size, which, own_q, other_q, far, far_c, far_r, maps, own_c, state, *rest
):
    keep, send, scores = rest[-2 * GROUP - 2], rest[-2 * GROUP - 1], rest[-2 * GROUP :]
    first = which[0] == 0
    for pair in range(GROUP):
        c = lanes_of(pair)
        query = jnp.where(first, other_q[:, c], own_q[0, 0, :, c])
        joint = joint_map(maps[pair], head_size)
        keys, values = memory_of(far[0, :, c], far[1, :, c], far_c[:, c], far_r[...], joint)
        part = scores[2 * pair : 2 * pair + 2]
        earlier = get_state(state, pair, head_size)
        sums, _ = attend_pair(query, keys, values, head_size, part, earlier)
        result = joined(sums, head_size)
        encoded = own_c[:, c]
        keep[0, 0, :, c] = jnp.where(first, encoded, result)
        send[:, c] = jnp.where(first, result, encoded)


def root_kernel(channels, *refs):
    total = None
    for c in refs[:-1]:
        x = c[...].astype(jnp.float32)
        part = jnp.sum(x * x, axis=1, keepdims=True)
        total = part if total is None else total + part
    refs[-1][...] = jnp.sqrt(total / channels + 1e-06)


def inner(queries, enc_keys_values, mem_map):
    heads, head_size = mem_map.shape[0], mem_map.shape[1]
    batches, rows, channels = (
        enc_keys_values.shape[0],
        enc_keys_values.shape[2],
        enc_keys_values.shape[3],
    )
    width = channels // CHUNKS
    segment = lax.axis_index("segment")
    size = lax.axis_size("ctx")
    swap = [(0, 1), (1, 0)]
    near_pairs = [(i, i ^ 1) for i in range(size)]
    far_pairs = [(i, (i + 1) % size if i % 2 else (i - 1) % size) for i in range(size)]
    which = segment.astype(jnp.int32)[None]

    def cut(array, index, chunk):
        start = (index,) + (0,) * (array.ndim - 2) + (chunk * width,)
        sizes = (1,) + array.shape[1:-1] + (width,)
        return lax.dynamic_slice(array, start, sizes)[0]

    own_queries = queries[0]
    near_kv, far_kv, other_q = [], [], []
    for g in range(CHUNKS):
        block = cut(enc_keys_values, segment, g)
        if GATE and g >= GATE:
            block, far_kv[g - GATE] = lax.optimization_barrier((block, far_kv[g - GATE]))
        far_kv.append(lax.ppermute(block, "ctx", far_pairs))
        near_kv.append(lax.ppermute(block, "ctx", near_pairs))
        other_q.append(lax.ppermute(cut(own_queries, 1 - segment, g), "segment", swap))

    step = GROUP * LANES
    steps = width // step

    tile = pl.BlockSpec((rows, step), lambda i, w: (0, i))
    pair_tile = pl.BlockSpec((2, rows, step), lambda i, w: (0, 0, i))
    root_tile = pl.BlockSpec((rows, 1), lambda i, w: (0, 0))
    state_tile = pl.BlockSpec((rows, 3 * step), lambda i, w: (0, i))
    state_shape = jax.ShapeDtypeStruct((rows, 3 * width), jnp.float32)
    chunk_shape = jax.ShapeDtypeStruct((rows, width), jnp.bfloat16)

    def call(kernel, blocks, operands, specs, out_shape, out_specs, aliases={}):
        return pl.pallas_call(
            functools.partial(kernel, head_size),
            out_shape=out_shape,
            grid_spec=pltpu.PrefetchScalarGridSpec(
                num_scalar_prefetch=1,
                grid=(steps,),
                in_specs=specs,
                out_specs=out_specs,
                scratch_shapes=[pltpu.VMEM((rows, blocks * rows), jnp.float32)] * (2 * GROUP),
            ),
            input_output_aliases=aliases,
            compiler_params=pltpu.CompilerParams(vmem_limit_bytes=VMEM_LIMIT),
            cost_estimate=pl.CostEstimate(
                flops=8 * rows * blocks * rows * width,
                bytes_accessed=8 * blocks * rows * width,
                transcendentals=rows * blocks * rows * width // head_size,
            ),
        )(which, *operands)

    def query_specs(g):
        base = g * steps
        return [
            pl.BlockSpec((1, 1, rows, step), lambda i, w: (0, w[0], 0, base + i)),
            tile,
        ]

    def own_spec(g):
        base = g * steps
        return pl.BlockSpec((1, 2, rows, step), lambda i, w: (w[0], 0, 0, base + i))

    def map_spec(g):
        base = g * steps
        return pl.BlockSpec((GROUP, LANES, LANES), lambda i, w: (base + i, 0, 0))

    own_c, near_c, far_c, states = [], [], [], []
    for g in range(CHUNKS):
        states.append(
            call(
                encode_near, 2,
                (queries, other_q[g], enc_keys_values, near_kv[g]),
                query_specs(g) + [own_spec(g), pair_tile],
                state_shape, state_tile,
            )
        )
    for g in range(CHUNKS):
        context = call(
            encode_far, 1,
            (queries, other_q[g], far_kv[g], states[g]),
            query_specs(g) + [pair_tile, state_tile],
            chunk_shape, tile,
        )
        own_c.append(context)
        far_c.append(lax.ppermute(context, "ctx", far_pairs))
        near_c.append(lax.ppermute(context, "ctx", near_pairs))

    def roots(contexts):
        return pl.pallas_call(
            functools.partial(root_kernel, channels),
            name="roots",
            out_shape=jax.ShapeDtypeStruct((rows, 1), jnp.float32),
        )(*contexts)

    maps = mem_map.reshape(heads // 2, LANES, 2 * head_size)
    own_r, near_r, far_r = roots(own_c), roots(near_c), roots(far_c)
    states = []
    for g in range(CHUNKS):
        states.append(
            call(
                decode_near, 2,
                (queries, other_q[g], enc_keys_values, near_kv[g], own_c[g], near_c[g])
                + (own_r, near_r, maps),
                query_specs(g)
                + [own_spec(g), pair_tile, tile, tile, root_tile, root_tile, map_spec(g)],
                state_shape, state_tile,
            )
        )

    def decode(g, final):
        base = g * steps
        operands = (
            queries, other_q[g], far_kv[g], far_c[g], far_r, maps, own_c[g], states[g],
        )
        specs = query_specs(g) + [pair_tile, tile, root_tile, map_spec(g), tile, state_tile]
        aliases = {}
        if final is not None:
            aliases = {len(operands) + 1: 0}
            operands += (final,)
            specs.append(pl.BlockSpec(memory_space=pl.ANY))
        return call(
            decode_far, 1, operands, specs,
            (jax.ShapeDtypeStruct((1, batches, rows, channels), jnp.bfloat16), chunk_shape),
            (pl.BlockSpec((1, 1, rows, step), lambda i, w: (0, w[0], 0, base + i)), tile),
            aliases,
        )

    final, arrived = None, []
    for g in range(CHUNKS):
        final, send = decode(g, final)
        arrived.append(lax.ppermute(send, "segment", swap))
    for g in range(CHUNKS):
        final = lax.dynamic_update_slice(
            final, arrived[g][None, None], (0, 1 - segment, 0, g * width)
        )
    return final


def solution(mesh):
    in_specs = (P("segment", None, "ctx", None), P(None, None, "ctx", None), P())
    out_specs = P("segment", None, "ctx", None)
    return jax.shard_map(inner, mesh=mesh, in_specs=in_specs, out_specs=out_specs, check_vma=False)
```
